32 devices in a mesh: ctx: 16 (over z, y, x), head: 2 (over core).
Axes of the slice: x: 2, y: 2, z: 4, core: 2. Of those that a mesh axis runs over, the one named last changes fastest.
Arguments:
- query_rows: bfloat16 [8192, 4096], P('ctx', 'head'), may hold values from -32 to 32
- key_rows: bfloat16 [8192, 1024], P('ctx', 'head'), may hold values from -32 to 32
- value_rows: bfloat16 [8192, 1024], P('ctx', 'head'), may hold values from -6 to 6
- out_weight: bfloat16 [4096, 4096], P('head', 'ctx'), may hold values from -0.71875 to 0.71875
Outputs:
- attended: bfloat16 [8192, 4096], P('ctx', 'head')
The draws below stay inside these ranges and needn't reach their ends.
All inputs are finite; a program needn't handle non-finite values.
Results may differ from the reference program's by a relative error of at most 0.015.
Values may be sent and summed in bfloat16 or wider, within the bound.
No kernel may reach another device: no remote copies, remote signals or barrier semaphores. Data moves between devices by JAX's collectives and lax.ppermute only.
A program may use at most 192 MiB of HBM per device.

```python
from functools import reduce
import jax
import jax.numpy as jnp
from jax import lax

D = 4096
QH = 32
KVH = 8
HD = 128
BLOCK = 512
TOKENS = 8192
N_HEAD = 2


def draw_key_rows(key, part):
    sample = jax.random.normal(jax.random.fold_in(key, 11), (TOKENS, KVH * HD), jnp.float32)
    sample = jnp.clip(sample, -6.0, 6.0)
    return sample.astype(jnp.bfloat16)


def draw_query_rows(key, part):
    sample = 2.0 * jax.random.normal(jax.random.fold_in(key, 12), (TOKENS, QH * HD), jnp.float32)
    sample = jnp.clip(sample, -12.0, 12.0)
    return sample.astype(jnp.bfloat16)


def steps_of(rng, extent, shards, smallest, top_value):
    def one(dim, parts):
        heights = jax.random.uniform(jax.random.fold_in(jax.random.fold_in(rng, 6), dim), (parts,), jnp.float32, smallest / len(shards), top_value / len(shards))
        return jnp.repeat(jnp.exp(heights), extent[dim] // parts).reshape((-1,) + (1,) * (len(extent) - dim - 1))

    loudness = one(*shards[0])
    for cut in shards[1:]:
        loudness = loudness * one(*cut)
    return loudness


def normal_values(stream_key, dims, scale, bound, split=(), held_as=jnp.bfloat16):
    level = steps_of(stream_key, dims, split, -0.22, 0.18) if split else 1.0
    values = jax.random.normal(stream_key, dims, jnp.float32) * scale * level
    return jnp.minimum(jnp.maximum(values, -bound), bound).astype(held_as)


def setup_inputs(seed: int = 0) -> dict:
    key_of = jax.random.split(jax.random.key(seed), 5)
    return {
        "query_rows": draw_query_rows(jax.random.fold_in(key_of[4], 71), 0),
        "key_rows": draw_key_rows(jax.random.fold_in(key_of[4], 71), 0),
        "value_rows": normal_values(key_of[2], (TOKENS, KVH * HD), 1.0, 6.0, ((0, 16), (1, 2))),
        "out_weight": normal_values(key_of[3], (QH * HD, D), 0.12, 0.71875, ((0, 2), (1, 16))),
    }


def block_stats(query, key_block, value_block):
    group = QH // KVH
    key_heads = jnp.repeat(key_block.astype(jnp.float32).reshape(BLOCK, KVH, HD), group, axis=1)
    value_heads = jnp.repeat(value_block.astype(jnp.float32).reshape(BLOCK, KVH, HD), group, axis=1)
    scores = jnp.einsum("qhd,khd->hqk", query, key_heads) * (HD ** -0.5)
    peak = jnp.max(scores, axis=-1)
    weights = jnp.exp(scores - peak[..., None])
    total = jnp.sum(weights, axis=-1)
    probs = weights.astype(jnp.bfloat16).astype(jnp.float32)
    partial_out = jnp.einsum("hqk,khd->hqd", probs, value_heads)
    return peak, total, partial_out


def reference(query_rows, key_rows, value_rows, out_weight):
    count_blocks = query_rows.shape[0] // BLOCK
    level_count = count_blocks.bit_length() - 1

    def attend_block(index):
        query = lax.dynamic_slice_in_dim(query_rows, index * BLOCK, BLOCK, 0)
        query = query.astype(jnp.float32).reshape(BLOCK, QH, HD)
        sources = [index] + [jnp.bitwise_xor(index, jnp.int32(1 << level)) for level in range(level_count)]
        pieces = []
        for source in sources:
            start = (source * BLOCK).astype(jnp.int32)
            key_block = lax.dynamic_slice_in_dim(key_rows, start, BLOCK, 0)
            value_block = lax.dynamic_slice_in_dim(value_rows, start, BLOCK, 0)
            pieces.append(block_stats(query, key_block, value_block))
        top = reduce(jnp.maximum, [piece[0] for piece in pieces])
        numer = sum(jnp.exp(piece[0] - top)[..., None] * piece[2] for piece in pieces)
        denom = sum(jnp.exp(piece[0] - top) * piece[1] for piece in pieces)
        hidden_block = (numer / denom[..., None]).transpose(1, 0, 2).reshape(BLOCK, QH * HD)
        return hidden_block.astype(jnp.bfloat16)

    hidden = lax.map(attend_block, jnp.arange(count_blocks, dtype=jnp.int32))
    hidden = hidden.reshape(query_rows.shape[0], QH * HD)
    width_group = QH * HD // N_HEAD
    mixed = jnp.zeros((query_rows.shape[0], D), jnp.float32)
    for group_index in range(N_HEAD):
        lower = group_index * width_group
        term = jnp.dot(hidden[:, lower:lower + width_group], out_weight[lower:lower + width_group],
                       preferred_element_type=jnp.float32)
        mixed = mixed + lax.optimization_barrier(term.astype(jnp.bfloat16)).astype(jnp.float32)
    return mixed.astype(jnp.bfloat16)
```

```python
import functools
import math

import jax
import jax.numpy as jnp
from jax import lax
from jax.experimental import pallas as pl
from jax.experimental.pallas import tpu as pltpu
from jax.sharding import PartitionSpec as P

HD = 128
BLOCK = 512


def from_partner(shard, axis, bit):
    return lax.ppermute(shard, axis, [(i, i ^ 1 << bit) for i in range(lax.axis_size(axis))])


def combine(state, update):
    peak_old, total_old, output_old = state
    peak_new, total_new, output_new = update
    top = jnp.maximum(peak_old, peak_new)
    scale_old = jnp.exp(peak_old - top)
    scale_new = jnp.exp(peak_new - top)
    total = scale_old * total_old + scale_new * total_new
    output = scale_old[..., None] * output_old + scale_new[..., None] * output_new
    return (top, total, output)


def plain_shards(query_rows, key_rows, value_rows, out_weight):
    tok_rows, query_cols = query_rows.shape
    block_count = tok_rows // BLOCK
    heads_kv = key_rows.shape[1] // HD
    heads_query = query_cols // HD
    group = heads_query // heads_kv
    queries = query_rows.reshape(block_count, BLOCK, heads_kv, group, HD)
    stacked = jnp.stack(
        [
            key_rows.reshape(block_count, BLOCK, heads_kv, HD),
            value_rows.reshape(block_count, BLOCK, heads_kv, HD),
        ]
    )
    factor = HD ** (-0.5)

    def block_stats(pair):
        scores = (
            jnp.einsum("bqgrd,bkgd->bgrqk", queries, pair[0], preferred_element_type=jnp.float32)
            * factor
        )
        peak = jnp.max(scores, axis=-1)
        weights = jnp.exp(scores - peak[..., None])
        total = jnp.sum(weights, axis=-1)
        probs = weights.astype(jnp.bfloat16)
        output = jnp.einsum("bgrqk,bkgd->bgrqd", probs, pair[1], preferred_element_type=jnp.float32)
        return (peak, total, output)

    state = block_stats(stacked)
    for level in range(lax.axis_size("ctx").bit_length() - 1):
        partner = from_partner(stacked, "ctx", level)
        state = combine(state, block_stats(partner))
    hidden = state[2] / state[1][..., None]
    hidden = hidden.transpose(0, 3, 1, 2, 4).reshape(tok_rows, query_cols).astype(jnp.bfloat16)
    terms = jnp.dot(
        hidden,
        lax.all_gather(out_weight, "ctx", axis=1, tiled=True),
        preferred_element_type=jnp.float32,
    )
    return lax.psum_scatter(terms.astype(jnp.bfloat16), "head", scatter_dimension=1, tiled=True)


def attend_body(blocks, tile, factor, query_ref, *refs):
    key_refs, value_refs, out_ref = refs[:blocks], refs[blocks : 2 * blocks], refs[2 * blocks]
    for start in range(0, query_ref.shape[0], tile):
        rows = slice(start, start + tile)
        query = query_ref[rows, :]
        scores = [
            lax.dot_general(
                query, key[...], (((1,), (1,)), ((), ())), preferred_element_type=jnp.float32
            )
            for key in key_refs
        ]
        peak = functools.reduce(
            jnp.maximum, [jnp.max(s, axis=-1, keepdims=True) for s in scores]
        )
        shift = peak * factor
        output, total = None, None
        for s, value in zip(scores, value_refs):
            weights = jnp.exp2(s * factor - shift)
            part = jnp.dot(
                weights.astype(jnp.bfloat16), value[...], preferred_element_type=jnp.float32
            )
            sums = jnp.sum(weights, axis=-1, keepdims=True)
            output = part if output is None else output + part
            total = sums if total is None else total + sums
        out_ref[rows, :] = (output / total).astype(out_ref.dtype)


def attend(query, key, value, partners, part, parts):
    rows = query.shape[0]
    heads_kv = key.shape[1] // HD // parts
    heads = query.shape[1] // HD // parts
    group = heads // heads_kv
    blocks = 1 + len(partners)
    block = (rows, HD)
    own = pl.BlockSpec(block, lambda j: (0, part * heads_kv + j // group))
    their_key = pl.BlockSpec(block, lambda j: (0, j // group))
    their_value = pl.BlockSpec(block, lambda j: (0, heads_kv + j // group))
    work = heads * rows * rows * blocks
    return pl.pallas_call(
        functools.partial(
            attend_body, blocks, min(256, rows), math.log2(math.e) * HD**-0.5
        ),
        out_shape=jax.ShapeDtypeStruct((rows, heads * HD), query.dtype),
        grid=(heads,),
        in_specs=[pl.BlockSpec(block, lambda j: (0, part * heads + j))]
        + [own]
        + [their_key] * len(partners)
        + [own]
        + [their_value] * len(partners),
        out_specs=pl.BlockSpec(block, lambda j: (0, j)),
        cost_estimate=pl.CostEstimate(
            flops=4 * work * HD, transcendentals=work, bytes_accessed=8 * rows * heads * HD
        ),
        compiler_params=pltpu.CompilerParams(
            dimension_semantics=("arbitrary",), vmem_limit_bytes=48 << 20
        ),
        name="attend",
    )(query, key, *partners, value, *partners)


def project_body(count, pick_ref, *refs):
    left, right, weights = refs[:count], refs[count : 2 * count], refs[2 * count : 2 * count + 4]
    out_ref, hidden, weight, sems, weight_sems = refs[2 * count + 4 :]
    half = left[0].shape[1]
    width = weights[0].shape[1]
    step = pl.program_id(0)

    def hidden_copies(r):
        return (
            pltpu.make_async_copy(left[r], hidden.at[r, :, pl.ds(0, half)], sems.at[r, 0]),
            pltpu.make_async_copy(right[r], hidden.at[r, :, pl.ds(half, half)], sems.at[r, 1]),
        )

    def weight_copy(source, e):
        return pltpu.make_async_copy(
            source, weight.at[:, pl.ds(e * width, width)], weight_sems.at[e]
        )

    @pl.when(step == 0)
    def _():
        for pair in range(2):

            @pl.when(pick_ref[0] == pair)
            def _():
                for e in range(2):
                    weight_copy(weights[2 * pair + e], e).start()

        for r in range(count):
            for copy in hidden_copies(r):
                copy.start()
        for e in range(2):
            weight_copy(weights[e], e).wait()

    for r in range(count):

        @pl.when(step == r)
        def _():
            for copy in hidden_copies(r):
                copy.wait()

    out_ref[0] = jnp.dot(
        hidden[step], weight[...], preferred_element_type=jnp.float32
    ).astype(out_ref.dtype)


def project(pick, left, right, weights):
    count = len(left)
    rows, half = left[0].shape
    depth, width = weights[0].shape
    anywhere = pl.BlockSpec(memory_space=pl.ANY)
    return pl.pallas_call(
        functools.partial(project_body, count),
        out_shape=jax.ShapeDtypeStruct((count, rows, 2 * width), left[0].dtype),
        grid=(count,),
        in_specs=[pl.BlockSpec(memory_space=pltpu.SMEM)] + [anywhere] * (2 * count + 4),
        out_specs=pl.BlockSpec((1, rows, 2 * width), lambda r: (r, 0, 0)),
        scratch_shapes=[
            pltpu.VMEM((count, rows, 2 * half), left[0].dtype),
            pltpu.VMEM((depth, 2 * width), left[0].dtype),
            pltpu.SemaphoreType.DMA((count, 2)),
            pltpu.SemaphoreType.DMA((2,)),
        ],
        cost_estimate=pl.CostEstimate(
            flops=4 * count * rows * depth * width,
            transcendentals=0,
            bytes_accessed=4 * (count * rows * half * 2 + depth * width * 2),
        ),
        compiler_params=pltpu.CompilerParams(
            dimension_semantics=("arbitrary",), vmem_limit_bytes=48 << 20
        ),
        name="project",
    )(pick, *left, *right, *weights)


def place_body(members, where_ref, *refs):
    pieces, out_ref = refs[:members], refs[members]
    width = pieces[0].shape[1] // 2
    for r in range(members):
        for e in range(2):
            slot = (e ^ where_ref[1]) * members + (r ^ where_ref[0])
            column = pl.multiple_of(slot * width, width)
            out_ref[:, pl.ds(column, width)] = pieces[r][:, e * width : (e + 1) * width]


def place(where, pieces):
    members = len(pieces)
    rows, cols = pieces[0].shape
    vmem = pl.BlockSpec(memory_space=pltpu.VMEM)
    return pl.pallas_call(
        functools.partial(place_body, members),
        out_shape=jax.ShapeDtypeStruct((rows, members * cols), pieces[0].dtype),
        in_specs=[pl.BlockSpec(memory_space=pltpu.SMEM)] + [vmem] * members,
        out_specs=vmem,
        cost_estimate=pl.CostEstimate(
            flops=0, transcendentals=0, bytes_accessed=4 * members * rows * cols
        ),
        compiler_params=pltpu.CompilerParams(vmem_limit_bytes=32 << 20),
        name="place",
    )(where, *pieces)


def quad_shards(query_rows, key_rows, value_rows, out_weight):
    size = lax.axis_size("ctx")
    me, core = lax.axis_index("ctx"), lax.axis_index("head")
    low, high = me & 3, me >> 2
    parts = 2
    cols = key_rows.shape[1] // parts

    def across(array, bits, keep=lambda i: True):
        return lax.ppermute(array, "ctx", [(i, i ^ bits) for i in range(size) if keep(i)])

    levels = [1 << level for level in range(size.bit_length() - 1)]
    partners = []
    for part in range(parts):
        own = jnp.concatenate(
            [key_rows[:, part * cols : (part + 1) * cols], value_rows[:, part * cols : (part + 1) * cols]],
            axis=1,
        )
        partners.append([across(own, bits) for bits in levels])

    middle = lambda i: (i >> 2) in (1, 2)
    near = across(out_weight, 4)
    far = across(out_weight, 8)
    inner = across(out_weight, 12, middle)
    outer = lax.ppermute(far, "ctx", [(i, i ^ 4) for i in range(size) if middle(i)])
    is_middle = (high == 1) | (high == 2)
    weights = [out_weight, near, far, jnp.where(is_middle, inner, outer)]

    left = attend(query_rows, key_rows, value_rows, partners[0], 0, parts)
    left_x, left_y = across(left, 1), across(left, 2)
    right = attend(query_rows, key_rows, value_rows, partners[1], 1, parts)
    right_y, right_x = across(right, 2), across(right, 1)
    left_xy, right_xy = across(left_x, 2), across(right_y, 1)
    lefts = [left, left_x, left_y, left_xy]
    rights = [right, right_x, right_y, right_xy]

    mine = core ^ (high >> 1)
    scalar = lambda value: jnp.reshape(value, (1,)).astype(jnp.int32)
    theirs = project(scalar(1 - mine), lefts, rights, weights)
    received = lax.ppermute(theirs, "head", [(0, 1), (1, 0)])
    kept = project(scalar(mine), lefts, rights, weights)
    sums = [
        (kept[r].astype(jnp.float32) + received[r].astype(jnp.float32)).astype(jnp.bfloat16)
        for r in range(4)
    ]
    pieces = [sums[0]] + [across(sums[r], r) for r in range(1, 4)]
    return place(jnp.stack([low, high & 1]).astype(jnp.int32), pieces)


def solution(mesh):
    placed = (P("ctx", "head"), P("ctx", "head"), P("ctx", "head"), P("head", "ctx"))

    def shards(query_rows, key_rows, value_rows, out_weight):
        heads_kv = key_rows.shape[1] // HD
        quads = (
            mesh.shape["ctx"] == 16
            and mesh.shape["head"] == 2
            and heads_kv % 2 == 0
            and query_rows.shape[0] == BLOCK
        )
        body = quad_shards if quads else plain_shards
        return body(query_rows, key_rows, value_rows, out_weight)

    return jax.shard_map(
        shards, mesh=mesh, in_specs=placed, out_specs=P("ctx", "head"), check_vma=False
    )
```

```python
import functools
import math

import jax
import jax.numpy as jnp
from jax import lax
from jax.experimental import pallas as pl
from jax.experimental.pallas import tpu as pltpu
from jax.sharding import PartitionSpec as P


HD = 128
BLOCK = 512


def from_partner(shard, axis, bit):
    return lax.ppermute(shard, axis, [(i, i ^ 1 << bit) for i in range(lax.axis_size(axis))])


def combine(state, update):
    peak_old, total_old, output_old = state
    peak_new, total_new, output_new = update
    top = jnp.maximum(peak_old, peak_new)
    scale_old = jnp.exp(peak_old - top)
    scale_new = jnp.exp(peak_new - top)
    total = scale_old * total_old + scale_new * total_new
    output = scale_old[..., None] * output_old + scale_new[..., None] * output_new
    return (top, total, output)


def plain_shards(query_rows, key_rows, value_rows, out_weight):
    tok_rows, query_cols = query_rows.shape
    block_count = tok_rows // BLOCK
    heads_kv = key_rows.shape[1] // HD
    heads_query = query_cols // HD
    group = heads_query // heads_kv
    queries = query_rows.reshape(block_count, BLOCK, heads_kv, group, HD)
    stacked = jnp.stack(
        [
            key_rows.reshape(block_count, BLOCK, heads_kv, HD),
            value_rows.reshape(block_count, BLOCK, heads_kv, HD),
        ]
    )
    factor = HD ** (-0.5)

    def block_stats(pair):
        scores = (
            jnp.einsum("bqgrd,bkgd->bgrqk", queries, pair[0], preferred_element_type=jnp.float32)
            * factor
        )
        peak = jnp.max(scores, axis=-1)
        weights = jnp.exp(scores - peak[..., None])
        total = jnp.sum(weights, axis=-1)
        probs = weights.astype(jnp.bfloat16)
        output = jnp.einsum("bgrqk,bkgd->bgrqd", probs, pair[1], preferred_element_type=jnp.float32)
        return (peak, total, output)

    state = block_stats(stacked)
    for level in range(lax.axis_size("ctx").bit_length() - 1):
        partner = from_partner(stacked, "ctx", level)
        state = combine(state, block_stats(partner))
    hidden = state[2] / state[1][..., None]
    hidden = hidden.transpose(0, 3, 1, 2, 4).reshape(tok_rows, query_cols).astype(jnp.bfloat16)
    terms = jnp.dot(
        hidden,
        lax.all_gather(out_weight, "ctx", axis=1, tiled=True),
        preferred_element_type=jnp.float32,
    )
    return lax.psum_scatter(terms.astype(jnp.bfloat16), "head", scatter_dimension=1, tiled=True)


def attend_body(blocks, factor, query_ref, *refs):
    key_refs, value_refs = refs[:blocks], refs[blocks : 2 * blocks]
    out_ref, keys, values, scores = refs[2 * blocks :]
    rows = query_ref.shape[0]
    heads = query_ref.shape[1] // HD
    spans = [slice(b * rows, (b + 1) * rows) for b in range(blocks)]
    for span, key, value in zip(spans, key_refs, value_refs):
        keys[span, :] = key[...]
        values[span, :HD] = value[...]
    values[:, HD:] = jnp.ones((blocks * rows, HD), values.dtype)

    def score(head):
        scores[head % 2] = lax.dot_general(
            query_ref[:, head * HD : (head + 1) * HD],
            keys[...],
            (((1,), (1,)), ((), ())),
            preferred_element_type=jnp.float32,
        )

    def finish(head):
        slot = head % 2
        peak = functools.reduce(jnp.maximum, [scores[slot, :, span] for span in spans])
        shift = jnp.max(peak, axis=-1, keepdims=True) * factor
        output = None
        for span in spans:
            weights = jnp.exp2(scores[slot, :, span] * factor - shift)
            part = jnp.dot(
                weights.astype(values.dtype), values[span, :], preferred_element_type=jnp.float32
            )
            output = part if output is None else output + part
        out_ref[:, head * HD : (head + 1) * HD] = (output[:, :HD] / output[:, HD:]).astype(
            out_ref.dtype
        )

    score(0)
    for head in range(heads):
        if head + 1 < heads:
            score(head + 1)
        finish(head)


def attend(query, key, value, partners, head):
    rows = query.shape[0]
    group = query.shape[1] // key.shape[1]
    blocks = 1 + len(partners)
    column = lambda place: pl.BlockSpec((rows, HD), lambda j: (0, place))
    work = group * rows * rows * blocks
    return pl.pallas_call(
        functools.partial(attend_body, blocks, math.log2(math.e) * HD**-0.5),
        out_shape=jax.ShapeDtypeStruct((rows, group * HD), query.dtype),
        grid=(1,),
        in_specs=[pl.BlockSpec((rows, group * HD), lambda j: (0, head)), column(head)]
        + [column(place) for _, place, _ in partners]
        + [column(head)]
        + [column(place) for _, _, place in partners],
        out_specs=pl.BlockSpec((rows, group * HD), lambda j: (0, 0)),
        scratch_shapes=[
            pltpu.VMEM((blocks * rows, HD), key.dtype),
            pltpu.VMEM((blocks * rows, 2 * HD), value.dtype),
            pltpu.VMEM((2, rows, blocks * rows), jnp.float32),
        ],
        cost_estimate=pl.CostEstimate(
            flops=4 * work * HD, transcendentals=work, bytes_accessed=8 * rows * group * HD
        ),
        compiler_params=pltpu.CompilerParams(
            dimension_semantics=("arbitrary",), vmem_limit_bytes=36 << 20
        ),
        name="attend",
    )(query, key, *[array for array, _, _ in partners], value, *[array for array, _, _ in partners])


def project_body(count, parts, choices, ready, pick_ref, *refs):
    hidden_parts = refs[: count * parts]
    refs = refs[count * parts :]
    sources, refs = refs[: sum(choices)], refs[sum(choices) :]
    ready_refs, outs = refs[:ready], refs[ready:-4]
    hidden, weight, sems, weight_sems = refs[-4:]
    part = hidden_parts[0].shape[1]
    width = sources[0].shape[1]
    step = pl.program_id(0)

    def hidden_copies(r):
        return [
            pltpu.make_async_copy(
                hidden_parts[r * parts + p],
                hidden.at[r, :, pl.ds(p * part, part)],
                sems.at[r, p],
            )
            for p in range(parts)
        ]

    @pl.when(step == 0)
    def _():
        def weight_copy(source, e):
            return pltpu.make_async_copy(
                source, weight.at[:, pl.ds(e * width, width)], weight_sems.at[e]
            )

        at = 0
        for e, options in enumerate(choices):
            for option in range(options):
                if options == 1:
                    weight_copy(sources[at], e).start()
                else:

                    @pl.when(pick_ref[0] == option)
                    def _():
                        weight_copy(sources[at], e).start()

                at += 1
        for r in range(count):
            for copy in hidden_copies(r):
                copy.start()
        for e in range(len(choices)):
            weight_copy(sources[0], e).wait()

    for r in range(count):

        @pl.when(step == r)
        def _():
            for copy in hidden_copies(r):
                copy.wait()

    product = jnp.dot(hidden[step], weight[...], preferred_element_type=jnp.float32)
    results = [ref[0].astype(jnp.float32) for ref in ready_refs] + [
        product[:, e * width : (e + 1) * width] for e in range(len(choices))
    ]
    if len(outs) == 1:
        outs[0][0] = results[0].astype(outs[0].dtype)
    else:
        first_mine = pick_ref[1] == 0
        outs[0][0] = jnp.where(first_mine, results[1], results[0]).astype(outs[0].dtype)
        outs[1][0] = jnp.where(first_mine, results[0], results[1]).astype(outs[1].dtype)


def project(pick, hidden, weights, ready=()):
    count, parts = len(hidden), len(hidden[0])
    rows, _ = hidden[0][0].shape
    depth, width = weights[0][0].shape
    kind = weights[0][0].dtype
    cols = len(weights) * width
    results = len(ready) + len(weights)
    sources = [source for options in weights for source in options]
    anywhere = pl.BlockSpec(memory_space=pl.ANY)
    block = pl.BlockSpec((1, rows, width), lambda r: (r, 0, 0))
    return pl.pallas_call(
        functools.partial(
            project_body, count, parts, [len(options) for options in weights], len(ready)
        ),
        out_shape=[jax.ShapeDtypeStruct((count, rows, width), kind)] * results,
        grid=(count,),
        in_specs=[pl.BlockSpec(memory_space=pltpu.SMEM)]
        + [anywhere] * (count * parts + len(sources))
        + [block] * len(ready),
        out_specs=[block] * results,
        scratch_shapes=[
            pltpu.VMEM((count, rows, depth), kind),
            pltpu.VMEM((depth, cols), kind),
            pltpu.SemaphoreType.DMA((count, parts)),
            pltpu.SemaphoreType.DMA((len(weights),)),
        ],
        cost_estimate=pl.CostEstimate(
            flops=2 * count * rows * depth * cols,
            transcendentals=0,
            bytes_accessed=2 * (count * rows * (depth + cols) + depth * cols),
        ),
        compiler_params=pltpu.CompilerParams(
            dimension_semantics=("arbitrary",), vmem_limit_bytes=32 << 20
        ),
        name="project",
    )(pick, *[piece for block_parts in hidden for piece in block_parts], *sources, *ready)


def place_body(members, where_ref, *refs):
    pieces, out_ref, sems = refs[:-2], refs[-2], refs[-1]
    width = pieces[0].shape[1]
    copies = []
    for e in range(2):
        for r in range(members):
            slot = (e ^ where_ref[1]) * members + (r ^ where_ref[0])
            column = pl.multiple_of(slot * width, width)
            copies.append(
                pltpu.make_async_copy(
                    pieces[e * members + r], out_ref.at[:, pl.ds(column, width)], sems.at[e, r]
                )
            )
    for copy in copies:
        copy.start()
    for copy in copies:
        copy.wait()


def place(where, pieces):
    members = len(pieces) // 2
    rows, width = pieces[0].shape
    return pl.pallas_call(
        functools.partial(place_body, members),
        out_shape=jax.ShapeDtypeStruct((rows, 2 * members * width), pieces[0].dtype),
        in_specs=[pl.BlockSpec(memory_space=pltpu.SMEM)]
        + [pl.BlockSpec(memory_space=pl.ANY)] * len(pieces),
        out_specs=pl.BlockSpec(memory_space=pltpu.VMEM),
        scratch_shapes=[pltpu.SemaphoreType.DMA((2, members))],
        cost_estimate=pl.CostEstimate(
            flops=0, transcendentals=0, bytes_accessed=8 * members * rows * width
        ),
        compiler_params=pltpu.CompilerParams(vmem_limit_bytes=16 << 20),
        name="place",
    )(where, *pieces)


PIECES = {1: 2, 2: 2, 4: 4, 8: 4}


def issue_order(parts):
    return sorted(
        ((bits, piece) for bits, count in PIECES.items() for piece in range(count)),
        key=lambda item: (item[1] * parts // PIECES[item[0]], -(item[0] == 4), -item[0]),
    )


def quad_shards(query_rows, key_rows, value_rows, out_weight):
    size = lax.axis_size("ctx")
    me, core = lax.axis_index("ctx"), lax.axis_index("head")
    low, high = me & 3, me >> 2
    parts = key_rows.shape[1] // HD

    def across(array, bits, keep=lambda i: True):
        return lax.ppermute(array, "ctx", [(i, i ^ bits) for i in range(size) if keep(i)])

    packed, arrived = {}, {}
    for bits, piece in issue_order(parts):
        count = PIECES[bits]
        if (count, piece) not in packed:
            span = slice(piece * parts // count * HD, (piece + 1) * parts // count * HD)
            packed[count, piece] = jnp.concatenate(
                [key_rows[:, span], value_rows[:, span]], axis=1
            )
        arrived[bits, piece] = across(packed[count, piece], bits)

    def partners(head):
        for bits, count in PIECES.items():
            piece = head * count // parts
            place = head - piece * parts // count
            yield arrived[bits, piece], place, parts // count + place

    middle = lambda i: (i >> 2) in (1, 2)
    near = across(out_weight, 4)
    far = across(out_weight, 8)
    inner = across(out_weight, 12, middle)
    outer = across(far, 4, middle)
    mine = core ^ (high >> 1)
    pick = jnp.stack([(high == 0) | (high == 3), mine]).astype(jnp.int32)

    hidden = [[None] * parts for _ in range(4)]
    for p in range(parts):
        hidden[0][p] = attend(query_rows, key_rows, value_rows, list(partners(p)), p)
        hidden[1][p] = across(hidden[0][p], 1)
        hidden[2][p] = across(hidden[0][p], 2)
        if p % 2 == 0:
            hidden[3][p] = across(hidden[1][p], 2)
        else:
            hidden[3][p] = across(hidden[2][p], 1)

    def finish(results):
        theirs, kept = results
        received = lax.ppermute(theirs, "head", [(0, 1), (1, 0)])
        sums = [
            (kept[r].astype(jnp.float32) + received[r].astype(jnp.float32)).astype(kept.dtype)
            for r in range(4)
        ]
        return [sums[0]] + [across(sums[r], r) for r in range(1, 4)]

    results = project(pick, hidden, [[out_weight], [far]])
    pieces = finish(results)
    ready = project(pick, hidden, [[near]])
    results = project(pick, hidden, [[inner, outer]], ready)
    pieces += finish(results)
    return place(jnp.stack([low, high & 1]).astype(jnp.int32), pieces)


def solution(mesh):
    placed = (P("ctx", "head"), P("ctx", "head"), P("ctx", "head"), P("head", "ctx"))
    quads = mesh.shape["ctx"] == 16 and mesh.shape["head"] == 2

    def shards(query_rows, key_rows, value_rows, out_weight):
        if not quads:
            return plain_shards(query_rows, key_rows, value_rows, out_weight)
        return quad_shards(query_rows, key_rows, value_rows, out_weight)

    return jax.shard_map(
        shards, mesh=mesh, in_specs=placed, out_specs=P("ctx", "head"), check_vma=False
    )
```

```python
import functools
import math

import jax
import jax.numpy as jnp
from jax import lax
from jax.experimental import pallas as pl
from jax.experimental.pallas import tpu as pltpu
from jax.sharding import PartitionSpec as P


HD = 128
BLOCK = 512


def from_partner(shard, axis, bit):
    return lax.ppermute(shard, axis, [(i, i ^ 1 << bit) for i in range(lax.axis_size(axis))])


def combine(state, update):
    peak_old, total_old, output_old = state
    peak_new, total_new, output_new = update
    top = jnp.maximum(peak_old, peak_new)
    scale_old = jnp.exp(peak_old - top)
    scale_new = jnp.exp(peak_new - top)
    total = scale_old * total_old + scale_new * total_new
    output = scale_old[..., None] * output_old + scale_new[..., None] * output_new
    return (top, total, output)


def plain_shards(query_rows, key_rows, value_rows, out_weight):
    tok_rows, query_cols = query_rows.shape
    block_count = tok_rows // BLOCK
    heads_kv = key_rows.shape[1] // HD
    heads_query = query_cols // HD
    group = heads_query // heads_kv
    queries = query_rows.reshape(block_count, BLOCK, heads_kv, group, HD)
    stacked = jnp.stack(
        [
            key_rows.reshape(block_count, BLOCK, heads_kv, HD),
            value_rows.reshape(block_count, BLOCK, heads_kv, HD),
        ]
    )
    factor = HD ** (-0.5)

    def block_stats(pair):
        scores = (
            jnp.einsum("bqgrd,bkgd->bgrqk", queries, pair[0], preferred_element_type=jnp.float32)
            * factor
        )
        peak = jnp.max(scores, axis=-1)
        weights = jnp.exp(scores - peak[..., None])
        total = jnp.sum(weights, axis=-1)
        probs = weights.astype(jnp.bfloat16)
        output = jnp.einsum("bgrqk,bkgd->bgrqd", probs, pair[1], preferred_element_type=jnp.float32)
        return (peak, total, output)

    state = block_stats(stacked)
    for level in range(lax.axis_size("ctx").bit_length() - 1):
        partner = from_partner(stacked, "ctx", level)
        state = combine(state, block_stats(partner))
    hidden = state[2] / state[1][..., None]
    hidden = hidden.transpose(0, 3, 1, 2, 4).reshape(tok_rows, query_cols).astype(jnp.bfloat16)
    terms = jnp.dot(
        hidden,
        lax.all_gather(out_weight, "ctx", axis=1, tiled=True),
        preferred_element_type=jnp.float32,
    )
    return lax.psum_scatter(terms.astype(jnp.bfloat16), "head", scatter_dimension=1, tiled=True)


def attend_body(blocks, factor, looped, _, query_ref, *refs):
    key_refs, value_refs = refs[:blocks], refs[blocks : 2 * blocks]
    out_ref, keys, values, scores = refs[2 * blocks :]
    rows = query_ref.shape[0]
    heads = query_ref.shape[1] // HD
    spans = [slice(b * rows, (b + 1) * rows) for b in range(blocks)]
    for span, key, value in zip(spans, key_refs, value_refs):
        keys[span, :] = key[...]
        values[span, :HD] = value[...]
    values[:, HD:] = jnp.ones((blocks * rows, HD), values.dtype)

    def columns(head):
        return pl.ds(pl.multiple_of(head * HD, HD), HD)

    def score(head, slot):
        scores[slot] = lax.dot_general(
            query_ref[:, columns(head)],
            keys[...],
            (((1,), (1,)), ((), ())),
            preferred_element_type=jnp.float32,
        )

    def finish(head, slot):
        peak = functools.reduce(jnp.maximum, [scores[slot, :, span] for span in spans])
        shift = jnp.max(peak, axis=-1, keepdims=True) * factor
        output = None
        for span in spans:
            weights = jnp.exp2(scores[slot, :, span] * factor - shift)
            part = jnp.dot(
                weights.astype(values.dtype), values[span, :], preferred_element_type=jnp.float32
            )
            output = part if output is None else output + part
        out_ref[:, columns(head)] = (output[:, :HD] / output[:, HD:]).astype(
            out_ref.dtype
        )

    score(0, 0)
    if looped:

        def two_heads(i, carry):
            score(2 * i + 1, 1)
            finish(2 * i, 0)
            score(jnp.minimum(2 * i + 2, heads - 1), 0)
            finish(2 * i + 1, 1)
            return carry

        lax.fori_loop(0, heads // 2, two_heads, 0)
    else:
        for head in range(heads):
            if head + 1 < heads:
                score(head + 1, (head + 1) % 2)
            finish(head, head % 2)


def attend(scalars, query, key, value, partners, head, looped=False):
    rows = query.shape[0]
    group = query.shape[1] // key.shape[1]
    blocks = 1 + len(partners)
    column = lambda place: pl.BlockSpec((rows, HD), lambda j: (0, place))
    work = group * rows * rows * blocks
    return pl.pallas_call(
        functools.partial(attend_body, blocks, math.log2(math.e) * HD**-0.5, looped),
        out_shape=jax.ShapeDtypeStruct((rows, group * HD), query.dtype),
        grid=(1,),
        in_specs=[
            pl.BlockSpec(memory_space=pltpu.SMEM),
            pl.BlockSpec((rows, group * HD), lambda j: (0, head)),
            column(head),
        ]
        + [column(place) for _, place, _ in partners]
        + [column(head)]
        + [column(place) for _, _, place in partners],
        out_specs=pl.BlockSpec((rows, group * HD), lambda j: (0, 0)),
        scratch_shapes=[
            pltpu.VMEM((blocks * rows, HD), key.dtype),
            pltpu.VMEM((blocks * rows, 2 * HD), value.dtype),
            pltpu.VMEM((2, rows, blocks * rows), jnp.float32),
        ],
        cost_estimate=pl.CostEstimate(
            flops=4 * work * HD, transcendentals=work, bytes_accessed=8 * rows * group * HD
        ),
        compiler_params=pltpu.CompilerParams(
            dimension_semantics=("arbitrary",), vmem_limit_bytes=18 << 20
        ),
        name="attend",
    )(scalars, query, key, *[array for array, _, _ in partners], value, *[array for array, _, _ in partners])


def project_body(count, parts, choices, ready, ordered, late, pick_ref, *refs):
    hidden_parts = refs[: count * parts]
    refs = refs[count * parts :]
    total = sum(len(rows) for options in choices for rows in options)
    source_refs, refs = refs[:total], refs[total:]
    ready_refs, outs = refs[:ready], refs[ready:-4]
    hidden, weight, sems, weight_sems = refs[-4:]
    part = hidden_parts[0].shape[1]
    width = source_refs[0].shape[1]
    step = pl.program_id(0)

    def hidden_copies(r):
        return [
            pltpu.make_async_copy(
                hidden_parts[r * parts + p],
                hidden.at[r, :, pl.ds(p * part, part)],
                sems.at[r, p],
            )
            for p in range(parts)
        ]

    @pl.when(step == 0)
    def _():
        sources = iter(source_refs)
        for e, options in enumerate(choices):
            columns = pl.ds(e * width, width)
            for option, rows in enumerate(options):
                copies, start = [], 0
                for size in rows:
                    target = weight.at[pl.ds(start, size), columns]
                    copies.append(pltpu.make_async_copy(next(sources), target, weight_sems.at[e]))
                    start += size
                if len(options) == 1:
                    for copy in copies:
                        copy.start()
                else:

                    @pl.when(pick_ref[0] == option)
                    def _():
                        for copy in copies:
                            copy.start()

        for r in range(count):
            for copy in hidden_copies(r):
                copy.start()
        for e in range(len(choices)):
            shard = weight.at[:, pl.ds(e * width, width)]
            pltpu.make_async_copy(shard, shard, weight_sems.at[e]).wait()

    for r in range(count):

        @pl.when(step == r)
        def _():
            for copy in hidden_copies(r):
                copy.wait()

    def order(results):
        if not ordered:
            return results
        first_mine = pick_ref[1] == 0
        return [
            jnp.where(first_mine, results[1], results[0]),
            jnp.where(first_mine, results[0], results[1]),
        ] + results[2:]

    def compute(columns, arrange):
        rows = hidden.shape[1]
        tile = rows if columns == 1 else rows // 2

        def some_rows(t, carry):
            span = pl.ds(pl.multiple_of(t * tile, tile), tile)
            product = jnp.dot(
                hidden[step, span, :],
                weight[:, : columns * width],
                preferred_element_type=jnp.float32,
            )
            fresh = [product[:, e * width : (e + 1) * width] for e in range(columns)]
            held = [ref[0, span, :].astype(jnp.float32) for ref in ready_refs]
            for out, result in zip(outs, order(arrange(fresh, held))):
                out[0, span, :] = result.astype(out.dtype)
            return carry

        lax.fori_loop(0, rows // tile, some_rows, 0)

    if late is None:
        compute(len(choices), lambda fresh, held: held[:1] + fresh + held[1:])
    else:
        @pl.when(step < late)
        def _():
            compute(1, lambda fresh, held: held[:1] + fresh + held[1:])

        @pl.when(step >= late)
        def _():
            compute(len(choices), lambda fresh, held: [fresh[1], fresh[0]] + fresh[2:])


def project(pick, hidden, weights, ready=(), ordered=True, late=None):
    count, parts = len(hidden), len(hidden[0])
    rows, _ = hidden[0][0].shape
    kind = weights[0][0][0].dtype
    width = weights[0][0][0].shape[1]
    depth = sum(span.shape[0] for span in weights[0][0])
    cols = len(weights) * width
    results = len(ready) + len(weights) if late is None else len(weights)
    choices = [[[span.shape[0] for span in source] for source in options] for options in weights]
    sources = [span for options in weights for source in options for span in source]
    anywhere = pl.BlockSpec(memory_space=pl.ANY)
    block = pl.BlockSpec((1, rows, width), lambda r: (r, 0, 0))
    return pl.pallas_call(
        functools.partial(
            project_body, count, parts, choices, len(ready), ordered, late
        ),
        out_shape=[jax.ShapeDtypeStruct((count, rows, width), kind)] * results,
        grid=(count,),
        in_specs=[pl.BlockSpec(memory_space=pltpu.SMEM)]
        + [anywhere] * (count * parts + len(sources))
        + [
            pl.BlockSpec((1, rows, width), lambda r, at=at: (at(r), 0, 0)) for _, at in ready
        ],
        out_specs=[block] * results,
        scratch_shapes=[
            pltpu.VMEM((count, rows, depth), kind),
            pltpu.VMEM((depth, cols), kind),
            pltpu.SemaphoreType.DMA((count, parts)),
            pltpu.SemaphoreType.DMA((len(weights),)),
        ],
        cost_estimate=pl.CostEstimate(
            flops=2 * count * rows * depth * cols,
            transcendentals=0,
            bytes_accessed=2 * (count * rows * (depth + cols) + depth * cols),
        ),
        compiler_params=pltpu.CompilerParams(
            dimension_semantics=("arbitrary",), vmem_limit_bytes=17 << 20
        ),
        name="project",
    )(pick, *[piece for block_parts in hidden for piece in block_parts], *sources, *[array for array, _ in ready])


def place_body(members, e, where_ref, *refs):
    pieces, (out_ref, held, sems) = refs[:members], refs[-3:]
    width = pieces[0].shape[1]
    loads, stores = [], []
    for r in range(members):
        slot = (e ^ where_ref[3]) * members + (r ^ where_ref[2])
        column = pl.multiple_of(slot * width, width)
        loads.append(pltpu.make_async_copy(pieces[r], held.at[r], sems.at[0, r]))
        stores.append(
            pltpu.make_async_copy(
                held.at[r], out_ref.at[:, pl.ds(column, width)], sems.at[1, r]
            )
        )
    for load in loads:
        load.start()
    for load, store in zip(loads, stores):
        load.wait()
        store.start()
    for store in stores:
        store.wait()


def place(where, e, pieces, placed=()):
    members = len(pieces)
    rows, width = pieces[0].shape
    anywhere = pl.BlockSpec(memory_space=pl.ANY)
    return pl.pallas_call(
        functools.partial(place_body, members, e),
        out_shape=jax.ShapeDtypeStruct((rows, 2 * members * width), pieces[0].dtype),
        in_specs=[pl.BlockSpec(memory_space=pltpu.SMEM)]
        + [anywhere] * (members + len(placed)),
        out_specs=anywhere,
        scratch_shapes=[
            pltpu.VMEM((members, rows, width), pieces[0].dtype),
            pltpu.SemaphoreType.DMA((2, members)),
        ],
        input_output_aliases={1 + members: 0} if placed else {},
        cost_estimate=pl.CostEstimate(
            flops=0, transcendentals=0, bytes_accessed=4 * members * rows * width
        ),
        compiler_params=pltpu.CompilerParams(vmem_limit_bytes=3 << 20),
        name="place",
    )(where, *pieces, *placed)


PIECES = {1: 2, 2: 2, 4: 4, 8: 4}


def issue_order(parts):
    return sorted(
        ((bits, piece) for bits, count in PIECES.items() for piece in range(count)),
        key=lambda item: (
            item[1] * parts // PIECES[item[0]] + (parts if item[1] and item[0] < 4 else 0),
            (4, 8, 2, 1).index(item[0]),
        ),
    )


def quad_shards(query_rows, key_rows, value_rows, out_weight):
    size = lax.axis_size("ctx")
    me, core = lax.axis_index("ctx"), lax.axis_index("head")
    low, high = me & 3, me >> 2
    parts = key_rows.shape[1] // HD

    def across(array, bits, keep=lambda i: True):
        return lax.ppermute(array, "ctx", [(i, i ^ bits) for i in range(size) if keep(i)])

    scalars = jnp.stack(
        [(high == 0) | (high == 3), core ^ (high >> 1), low, high & 1]
    ).astype(jnp.int32)
    key_rows, value_rows, scalars = lax.optimization_barrier((key_rows, value_rows, scalars))

    packed, arrived = {}, {}
    for bits, piece in issue_order(parts):
        count = PIECES[bits]
        if (count, piece) not in packed:
            span = slice(piece * parts // count * HD, (piece + 1) * parts // count * HD)
            packed[count, piece] = jnp.concatenate(
                [key_rows[:, span], value_rows[:, span]], axis=1
            )
        arrived[bits, piece] = across(packed[count, piece], bits)

    def partners(head):
        for bits, count in PIECES.items():
            piece = head * count // parts
            place = head - piece * parts // count
            yield arrived[bits, piece], place, parts // count + place

    middle = lambda i: (i >> 2) in (1, 2)
    half = out_weight.shape[0] // 2
    near = across(out_weight, 4)
    far = [across(out_weight[h * half : (h + 1) * half], 8) for h in range(2)]
    inner = across(out_weight, 12, middle)
    outer = [across(far[h], 4, middle) for h in range(2)]
    hidden = [[None] * parts for _ in range(4)]
    for p in range(parts):
        hidden[0][p] = attend(
            scalars,
            query_rows,
            key_rows,
            value_rows,
            list(partners(p)),
            p,
            looped=p == parts - 1 and query_rows.shape[1] // HD // parts % 2 == 0,
        )
        hidden[1][p] = across(hidden[0][p], 1)
        hidden[2][p] = across(hidden[0][p], 2)
        if p % 2 == 0:
            hidden[3][p] = across(hidden[1][p], 2)
        else:
            hidden[3][p] = across(hidden[2][p], 1)

    def swap(theirs):
        return lax.ppermute(theirs, "head", [(0, 1), (1, 0)])

    def send(kept, received, blocks):
        sums = [
            (kept[n].astype(jnp.float32) + received[n].astype(jnp.float32)).astype(kept.dtype)
            for n in range(len(blocks))
        ]
        return {r: across(total, r) if r else total for r, total in zip(blocks, sums)}

    everyone = (0, 1, 2, 3)
    ready = project(scalars, hidden[:3], [[[out_weight]], [[near]]], ordered=False)
    early = lambda r: jnp.minimum(r, 2)
    theirs, kept, done = project(
        scalars,
        hidden,
        [[far], [[out_weight]], [[near]]],
        [(array, early) for array in ready],
        late=3,
    )
    first = send(kept, swap(theirs), everyone)

    second = {}
    for blocks in ((3, 1), (2, 0)):
        at = lambda r, blocks=blocks: blocks[0] + r * (blocks[1] - blocks[0])
        theirs, kept = project(
            scalars, [hidden[r] for r in blocks], [[[inner], outer]], [(done, at)]
        )
        second.update(send(kept, swap(theirs), blocks))

    placed = place(scalars, 0, [first[r] for r in everyone])
    return place(scalars, 1, [second[r] for r in everyone], [placed])


def solution(mesh):
    placed = (P("ctx", "head"), P("ctx", "head"), P("ctx", "head"), P("head", "ctx"))
    quads = mesh.shape["ctx"] == 16 and mesh.shape["head"] == 2

    def shards(query_rows, key_rows, value_rows, out_weight):
        if not quads:
            return plain_shards(query_rows, key_rows, value_rows, out_weight)
        return quad_shards(query_rows, key_rows, value_rows, out_weight)

    return jax.shard_map(
        shards, mesh=mesh, in_specs=placed, out_specs=P("ctx", "head"), check_vma=False
    )
```
